512 devices in a mesh: dp: 32 (over y_hi, z), rep: 16 (over x, y_lo, core).
Axes of the slice: x: 4, y: 4 (y_hi: 2, y_lo: 2; y = y_hi * 2 + y_lo), z: 16, core: 2. Of those that a mesh axis runs over, the one named last changes fastest.
Arguments:
- mentions: bfloat16 [65536, 1024], P(('dp', 'rep')), may hold values from -48 to 48
- entity_states: bfloat16 [65536, 1024], P(('dp', 'rep')), may hold values from -8 to 8
- head: bfloat16 [1024, 1024], P('dp'), may hold values from -4 to 4
Outputs:
- pair_loss: float32 [65536], P(('dp', 'rep'))
- mention_grad: bfloat16 [65536, 1024], P(('dp', 'rep'))
- state_grad: bfloat16 [65536, 1024], P(('dp', 'rep'))
The draws below stay inside these ranges and needn't reach their ends.
All inputs are finite; a program needn't handle non-finite values.
Results may differ from the reference program's by a relative error of at most 0.0073.
Values may be sent and summed in bfloat16 or wider, within the bound.
A program may use at most 64 MiB of HBM per device.

```python
import math
import jax
import jax.numpy as jnp
from jax import lax

D = 1024
GROUP = 2048
TOKENS = 65536


def entity_draw(key):
    base_states = jnp.clip(jax.random.normal(jax.random.fold_in(key, 11), (TOKENS, D), jnp.float32), -6.0, 6.0)
    return base_states


def draw_entity_states(key, part):
    return entity_draw(key).astype(jnp.bfloat16)


def draw_mentions(key, part):
    queries = jnp.clip(jax.random.normal(jax.random.fold_in(key, 21), (TOKENS, D), jnp.float32), -6.0, 6.0)
    return queries.astype(jnp.bfloat16)


def draw_head(key, part):
    noise = jnp.clip(jax.random.normal(jax.random.fold_in(key, 31), (D, D), jnp.float32), -6.0, 6.0)
    return (jnp.eye(D, dtype=jnp.float32) + 0.5 / math.sqrt(D) * noise).astype(jnp.bfloat16)


def setup_inputs(seed: int = 0) -> dict:
    streams_of = jax.random.split(jax.random.key(seed), 4)
    return {
        "mentions": draw_mentions(jax.random.fold_in(streams_of[3], 71), 0),
        "entity_states": draw_entity_states(jax.random.fold_in(streams_of[3], 71), 0),
        "head": draw_head(jax.random.fold_in(streams_of[3], 71), 0),
    }


def reference(mentions, entity_states, head):
    scale_factor = 3.0 / math.sqrt(D)
    projected = jnp.dot(entity_states, head, preferred_element_type=jnp.float32).astype(jnp.bfloat16)
    groups = TOKENS // GROUP
    mention_blocks = mentions.reshape(groups, GROUP, D)
    entity_blocks = projected.reshape(groups, GROUP, D)

    def per_group(operands):
        mention_blk, entity_blk = operands
        scores = jnp.dot(mention_blk, entity_blk.T, preferred_element_type=jnp.float32) * scale_factor
        row_max = lax.optimization_barrier(jnp.max(scores, axis=1))
        log_total = row_max + jnp.log(lax.optimization_barrier(jnp.sum(jnp.exp(scores - row_max[:, None]), axis=1)))
        chances = jnp.exp(scores - log_total[:, None]).astype(jnp.bfloat16)
        grad_m = scale_factor * (jnp.dot(chances, entity_blk, preferred_element_type=jnp.float32) - entity_blk.astype(jnp.float32))
        grad_e = scale_factor * (jnp.dot(chances.T, mention_blk, preferred_element_type=jnp.float32) - mention_blk.astype(jnp.float32))
        pair_loss = log_total - jnp.diagonal(scores)
        return (pair_loss, grad_m.astype(jnp.bfloat16), grad_e.astype(jnp.bfloat16))
    pair_loss, grad_m, grad_e = lax.map(per_group, (mention_blocks, entity_blocks))
    state_grad = jnp.dot(grad_e.reshape(TOKENS, D), head.T, preferred_element_type=jnp.float32).astype(jnp.bfloat16)
    return (pair_loss.reshape(TOKENS), grad_m.reshape(TOKENS, D), state_grad)
```

```python
import functools
import math

import jax
import jax.numpy as jnp
from jax import lax
from jax.experimental import pallas as pl
from jax.experimental.pallas import tpu as pltpu
from jax.sharding import Mesh
from jax.sharding import PartitionSpec as P

DP_REP = ("dp_0", "dp_1", "rep_0", "rep_1", "rep_2")
MESH = pl.DeviceIdType.MESH
NX, NY, NC = 4, 2, 2
RANKS = NX * NY * NC
CHUNK = 256
NT = (((1,), (1,)), ((), ()))


def kernel(
    nz, scale,
    m_ref, e_ref, h_ref,
    loss_ref, mg_ref, sg_ref,
    m_all, p_all, h_all, e_v, acc, st, ct, lse, lt, dp, out_v,
    local_sem, m_recv, m_sib, p_recv, p_sib, hz_recv, hy_recv, h_sib, st_recv,
    m_send, p_send, h_send, st_send, out_sem,
):
    rows, width = m_ref.shape
    half = rows // 2
    shard = h_ref.shape[0]
    part = shard // NC
    group = rows * RANKS
    yh, z = lax.axis_index("dp_0"), lax.axis_index("dp_1")
    x, y, c = lax.axis_index("rep_0"), lax.axis_index("rep_1"), lax.axis_index("rep_2")
    xa, xb, x2 = lax.rem(x + 1 + 2 * c, NX), lax.rem(x + 3 - 2 * c, NX), lax.rem(x + 2, NX)
    yo, co = 1 - y, 1 - c
    rank = x * 4 + y * 2 + c
    ahead, behind, across, sibling = {"rep_0": xa}, {"rep_0": xb}, {"rep_1": yo}, {"rep_2": co}
    up, down = {"dp_1": lax.rem(z + 1, nz)}, {"dp_1": lax.rem(z + nz - 1, nz)}
    partner = {"dp_0": 1 - yh, "rep_1": yo}

    def peer(k):
        return {
            "rep_0": lax.rem(x + k // 4, NX),
            "rep_1": lax.rem(y + (k // 2) % 2, NY),
            "rep_2": lax.rem(c + k % 2, NC),
        }

    barrier = pltpu.get_barrier_semaphore()
    for device in [up, down, partner] + [peer(k) for k in range(1, RANKS)]:
        pl.semaphore_signal(barrier, inc=1, device_id=device, device_id_type=MESH)
    own = pl.ds(pl.multiple_of(rank * rows, rows), rows)
    own_shard = pl.ds(pl.multiple_of((yh * nz + z) * shard, shard), shard)
    fills = [
        pltpu.make_async_copy(m_ref, m_all.at[own], local_sem.at[0]),
        pltpu.make_async_copy(e_ref, e_v, local_sem.at[1]),
        pltpu.make_async_copy(h_ref, h_all.at[own_shard], local_sem.at[2]),
    ]
    for fill in fills:
        fill.start()
    pl.semaphore_wait(barrier, RANKS + 2)

    def copy(src, dst, send_sem, recv_sem, device):
        return pltpu.make_async_remote_copy(
            src_ref=src, dst_ref=dst, send_sem=send_sem, recv_sem=recv_sem,
            device_id=device, device_id_type=MESH,
        )

    def place(cx, cy, core, piece):
        return pl.ds(pl.multiple_of((cx * 4 + cy * 2 + core) * rows + piece * half, half), half)

    def index(cx, cy, piece):
        return piece * (NX * NY) + cx * NY + cy

    def spread(array, send_sem, recv, sib, each_sib, source=None):
        def src(cx, cy, piece):
            if source is not None:
                return source.at[pl.ds(piece * half, half)]
            return array.at[place(cx, cy, c, piece)]

        def to(device, cx, cy, piece):
            copy(
                src(cx, cy, piece), array.at[place(cx, cy, c, piece)],
                send_sem, recv.at[index(cx, cy, piece)], device,
            ).start()

        def to_sib(cx, cy, piece):
            copy(
                src(cx, cy, piece), array.at[place(cx, cy, c, piece)],
                send_sem, sib.at[index(cx, cy, piece)] if each_sib else sib, sibling,
            ).start()

        def got(cx, cy, piece):
            here = array.at[place(cx, cy, c, piece)]
            copy(here, here, send_sem, recv.at[index(cx, cy, piece)], sibling).wait_recv()

        return to, to_sib, got

    A, B = 0, 1

    def relays(array, send_sem, recv, sib, each_sib):
        to, to_sib, got = spread(array, send_sem, recv, sib, each_sib)

        def step(cx, cy, piece, *devices):
            got(cx, cy, piece)
            for device in devices:
                to(device, cx, cy, piece)
            to_sib(cx, cy, piece)

        def one():
            step(xb, y, A, ahead, across)
            step(x, yo, B, ahead, behind)
            step(xa, y, A, across)

        def two():
            step(x, yo, A)
            step(xa, y, B, behind)
            step(xb, y, B)

        def three():
            step(x2, y, A, across)
            step(xb, yo, B, ahead)
            step(xb, yo, A)
            step(xa, yo, A)
            step(xa, yo, B)

        def four():
            step(x2, y, B)
            step(x2, yo, A)
            step(x2, yo, B)

        return one, two, three, four

    def h_place(cy, cz):
        return pl.ds(pl.multiple_of((cy * nz + cz) * shard + c * part, part), part)

    def h_to(device, recv, cy, cz, source=None):
        here = h_all.at[h_place(cy, cz)]
        src = here if source is None else source.at[pl.ds(pl.multiple_of(c * part, part), part)]
        copy(src, here, h_send, recv, device).start()

    def h_got(recv, cy, cz):
        here = h_all.at[h_place(cy, cz)]
        copy(here, here, h_send, recv, sibling).wait_recv()

    h_to(up, hz_recv.at[z], yh, z, h_ref)
    h_to(down, hz_recv.at[z], yh, z, h_ref)
    h_to(partner, hy_recv.at[z], yh, z, h_ref)
    to, to_sib, _ = spread(m_all, m_send, m_recv, m_sib, False, m_ref)
    to(across, x, y, B)
    to(ahead, x, y, A)
    to(behind, x, y, A)
    to(across, x, y, A)
    to(ahead, x, y, B)
    to(behind, x, y, B)
    to_sib(x, y, A)
    to_sib(x, y, B)
    m_one, m_two, m_three, m_four = relays(m_all, m_send, m_recv, m_sib, False)

    ups = nz // 2
    downs = nz - 1 - ups

    def crossed(cz):
        h_got(hy_recv.at[cz], 1 - yh, cz)
        h_to(sibling, h_sib.at[1], 1 - yh, cz)

    order = []
    order.append(z)
    for step in range(ups):
        cz = lax.rem(z + nz - 1 - step, nz)
        h_got(hz_recv.at[cz], yh, cz)
        if step < ups - 1:
            h_to(up, hz_recv.at[cz], yh, cz)
        h_to(partner, hy_recv.at[cz], yh, cz)
        h_to(sibling, h_sib.at[0], yh, cz)
        order.append(cz)
        if step < downs:
            cz = lax.rem(z + 1 + step, nz)
            h_got(hz_recv.at[cz], yh, cz)
            if step < downs - 1:
                h_to(down, hz_recv.at[cz], yh, cz)
            h_to(partner, hy_recv.at[cz], yh, cz)
            h_to(sibling, h_sib.at[0], yh, cz)
            order.append(cz)
        if step == 2:
            m_one()
        if step == 4:
            m_two()
        if step == 6:
            m_three()
        if step >= 2:
            for cz in order[2 * step - 4 : 2 * step - 2]:
                crossed(cz)
    for cz in order[2 * ups - 4 :]:
        crossed(cz)
    for fill in fills:
        fill.wait()

    def all_of(ref, count, send_sem, recv_sem):
        view = ref.at[pl.ds(0, count)]
        return copy(view, view, send_sem, recv_sem, sibling)

    def columns(n):
        return pl.ds(pl.multiple_of(n * CHUNK, CHUNK), CHUNK)

    def project(cy, first):
        side = nz * shard
        at = pl.ds(pl.multiple_of(cy * side, side), side)

        @pl.loop(0, width // CHUNK)
        def _(n):
            term = jnp.dot(e_v[:, at], h_all[at, columns(n)], preferred_element_type=jnp.float32)
            if first:
                acc[:, columns(n)] = term
            else:
                total = (acc[:, columns(n)] + term).astype(jnp.bfloat16)
                p_all[own, columns(n)] = total
                acc[:, columns(n)] = -total.astype(jnp.float32)

    all_of(h_all, (nz - 1) * part, h_send, h_sib.at[0]).wait_recv()
    project(yh, True)
    all_of(h_all, nz * part, h_send, h_sib.at[1]).wait_recv()
    project(1 - yh, False)

    to, to_sib, _ = spread(p_all, p_send, p_recv, p_sib, True)
    to(across, x, y, B)
    to(ahead, x, y, A)
    to(behind, x, y, A)
    to_sib(x, y, A)
    to_sib(x, y, B)
    p_one, p_two, p_three, p_four = relays(p_all, p_send, p_recv, p_sib, True)

    m_four()
    all_of(m_all, group // NC, m_send, m_sib).wait_recv()

    @pl.loop(0, group // CHUNK)
    def _(n):
        at = pl.ds(pl.multiple_of(n * CHUNK, CHUNK), CHUNK)
        scores = scale * lax.dot_general(
            p_all[own, :], m_all[at, :], NT, preferred_element_type=jnp.float32
        )
        st[:, at] = scores
        top = jnp.max(scores, axis=0, keepdims=True)
        lse[rank, :, at] = top + jnp.log(jnp.sum(jnp.exp(scores - top), axis=0, keepdims=True))

    for k in range(1, RANKS):
        copy(lse.at[rank], lse.at[rank], st_send, st_recv.at[rank], peer(k)).start()
    to(across, x, y, A)
    to(ahead, x, y, B)
    to(behind, x, y, B)
    p_one()
    for k in range(1, RANKS):
        device = peer(k)
        other = device["rep_0"] * 4 + device["rep_1"] * 2 + device["rep_2"]
        copy(lse.at[other], lse.at[other], st_send, st_recv.at[other], sibling).wait_recv()
    parts = lse[...]
    top = jnp.max(parts, axis=0)
    lt[...] = top + jnp.log(jnp.sum(jnp.exp(parts - top[None]), axis=0))

    @pl.loop(0, group // CHUNK)
    def _(n):
        at = pl.ds(pl.multiple_of(n * CHUNK, CHUNK), CHUNK)
        ct[:, at] = jnp.exp(st[:, at] - lt[:, at]).astype(jnp.bfloat16)

    block = st[:, own]
    diagonal = lax.broadcasted_iota(jnp.int32, block.shape, 0) == lax.broadcasted_iota(
        jnp.int32, block.shape, 1
    )
    own_total = lt[:, own]
    loss_ref[...] = own_total - jnp.sum(jnp.where(diagonal, block, 0.0), axis=0, keepdims=True)
    total_rows = jnp.broadcast_to(own_total, (rows, rows)).T[:, :1]
    p_two()

    @pl.loop(0, width // CHUNK)
    def _(n):
        total = jnp.dot(ct[...], m_all[:, columns(n)], preferred_element_type=jnp.float32)
        total = total - m_all[own, columns(n)].astype(jnp.float32)
        dp[:, columns(n)] = (scale * total).astype(jnp.bfloat16)

    p_three()

    @pl.loop(0, width // CHUNK)
    def _(n):
        grad = lax.dot_general(dp[...], h_all[columns(n), :], NT, preferred_element_type=jnp.float32)
        out_v[1, :, columns(n)] = grad.astype(jnp.bfloat16)

    put_state = pltpu.make_async_copy(out_v.at[1], sg_ref, out_sem.at[0])
    put_state.start()

    def chip(cx, cy):
        for piece in (A, B):
            here = p_all.at[place(cx, cy, co, piece)]
            copy(here, here, p_send, p_sib.at[index(cx, cy, piece)], sibling).wait_recv()
        at = pl.ds(pl.multiple_of((cx * 4 + cy * 2) * rows, NC * rows), NC * rows)
        scores = scale * lax.dot_general(
            m_all[own, :], p_all[at, :], NT, preferred_element_type=jnp.float32
        )
        share = jnp.exp(scores - total_rows).astype(jnp.bfloat16)

        @pl.loop(0, width // CHUNK)
        def _(n):
            acc[:, columns(n)] += jnp.dot(
                share, p_all[at, columns(n)], preferred_element_type=jnp.float32
            )

    chip(x, y)
    chip(x, yo)
    chip(xa, y)
    chip(xb, y)
    p_four()
    chip(x2, y)
    chip(xa, yo)
    chip(xb, yo)
    chip(x2, yo)

    @pl.loop(0, width // CHUNK)
    def _(n):
        out_v[0, :, columns(n)] = (scale * acc[:, columns(n)]).astype(jnp.bfloat16)

    put_mention = pltpu.make_async_copy(out_v.at[0], mg_ref, out_sem.at[1])
    put_mention.start()
    sent = 9 + 5 + 2 * NX * NY
    all_of(m_all, sent * half, m_send, m_sib).wait_send()
    all_of(p_all, sent * half, p_send, m_sib).wait_send()
    pieces = (nz - 1) + nz + (nz - 1) + nz
    all_of(h_all, pieces * part, h_send, m_sib).wait_send()
    view = lse.at[pl.ds(0, RANKS - 1)]
    copy(view, view, st_send, m_sib, sibling).wait_send()
    put_state.wait()
    put_mention.wait()


def local(nz, mentions, entity_states, head):
    rows, width = mentions.shape
    group = rows * RANKS
    bf16, f32 = jnp.bfloat16, jnp.float32
    pieces = 2 * NX * NY
    dma = pltpu.SemaphoreType.DMA
    any_spec = pl.BlockSpec(memory_space=pl.ANY)
    loss, mention_grad, state_grad = pl.pallas_call(
        functools.partial(kernel, nz, 3.0 / math.sqrt(width)),
        out_shape=(
            jax.ShapeDtypeStruct((1, rows), f32),
            jax.ShapeDtypeStruct((rows, width), bf16),
            jax.ShapeDtypeStruct((rows, width), bf16),
        ),
        in_specs=[any_spec] * 3,
        out_specs=(pl.BlockSpec(memory_space=pltpu.VMEM), any_spec, any_spec),
        scratch_shapes=[
            pltpu.VMEM((group, width), bf16),
            pltpu.VMEM((group, width), bf16),
            pltpu.VMEM((width, width), bf16),
            pltpu.VMEM((rows, width), bf16),
            pltpu.VMEM((rows, width), f32),
            pltpu.VMEM((rows, group), f32),
            pltpu.VMEM((rows, group), bf16),
            pltpu.VMEM((RANKS, 1, group), f32),
            pltpu.VMEM((1, group), f32),
            pltpu.VMEM((rows, width), bf16),
            pltpu.VMEM((2, rows, width), bf16),
            dma((3,)),
            dma((pieces,)),
            dma,
            dma((pieces,)),
            dma((pieces,)),
            dma((nz,)),
            dma((nz,)),
            dma((2,)),
            dma((RANKS,)),
            dma, dma, dma, dma,
            dma((2,)),
        ],
        compiler_params=pltpu.CompilerParams(collective_id=0, has_side_effects=True),
    )(mentions, entity_states, head)
    return loss.reshape(rows), mention_grad, state_grad


def solution(mesh):
    torus = Mesh(mesh.devices.reshape(2, 16, 4, 2, 2), DP_REP)
    in_specs = (P(DP_REP, None), P(DP_REP, None), P(("dp_0", "dp_1"), None))
    out_specs = (P(DP_REP), P(DP_REP, None), P(DP_REP, None))
    return jax.shard_map(
        functools.partial(local, 16), mesh=torus, in_specs=in_specs, out_specs=out_specs, check_vma=False
    )
```

```python
import functools
import math

import jax
import jax.numpy as jnp
from jax import lax
from jax.experimental import pallas as pl
from jax.experimental.pallas import tpu as pltpu
from jax.sharding import Mesh
from jax.sharding import PartitionSpec as P

DP_REP = ("dp_0", "dp_1", "rep_0", "rep_1", "rep_2")
MESH = pl.DeviceIdType.MESH
NX, NY, NC = 4, 2, 2
RANKS = NX * NY * NC
CHUNK = 256
NT = (((1,), (1,)), ((), ()))


def kernel(
    nz, scale,
    m_ref, e_ref, h_ref,
    loss_ref, mg_ref, sg_ref,
    m_all, e_all, p_all, h_all, acc, st, ct, lse, lt, dp,
    local_sem, m_recv, m_sib, e_recv, p_sib, hz_recv, hy_recv, h_sib, st_recv,
    m_send, e_send, p_send, h_send, st_send,
):
    rows, width = m_ref.shape
    half = rows // 2
    shard = h_ref.shape[0]
    part = shard // NC
    group = rows * RANKS
    yh, z = lax.axis_index("dp_0"), lax.axis_index("dp_1")
    x, y, c = lax.axis_index("rep_0"), lax.axis_index("rep_1"), lax.axis_index("rep_2")
    xa, xb, x2 = lax.rem(x + 1 + 2 * c, NX), lax.rem(x + 3 - 2 * c, NX), lax.rem(x + 2, NX)
    yo, co = 1 - y, 1 - c
    rank = x * 4 + y * 2 + c
    ahead, behind, across, sibling = {"rep_0": xa}, {"rep_0": xb}, {"rep_1": yo}, {"rep_2": co}
    partner = {"dp_0": 1 - yh, "rep_1": yo}

    def zat(d):
        return lax.rem(z + nz + d * (1 - 2 * c), nz)

    def along(d):
        return {"dp_1": zat(d)}

    def peer(k):
        return {
            "rep_0": lax.rem(x + k // 4, NX),
            "rep_1": lax.rem(y + (k // 2) % 2, NY),
            "rep_2": lax.rem(c + k % 2, NC),
        }

    barrier = pltpu.get_barrier_semaphore()
    friends = [along(d) for d in (4, -4, 2, -2, 1, -1)] + [partner]
    friends += [peer(k) for k in range(1, RANKS)]
    for device in friends:
        pl.semaphore_signal(barrier, inc=1, device_id=device, device_id_type=MESH)
    own = pl.ds(pl.multiple_of(rank * rows, rows), rows)
    own_chip = pl.ds(pl.multiple_of((x * NY + y) * rows, rows), rows)
    own_shard = pl.ds(pl.multiple_of((yh * nz + z) * shard, shard), shard)
    fills = [
        pltpu.make_async_copy(m_ref, m_all.at[own], local_sem.at[0]),
        pltpu.make_async_copy(e_ref, e_all.at[own_chip], local_sem.at[1]),
        pltpu.make_async_copy(h_ref, h_all.at[own_shard], local_sem.at[2]),
    ]
    for fill in fills:
        fill.start()
    pl.semaphore_wait(barrier, len(friends))

    def copy(src, dst, send_sem, recv_sem, device):
        return pltpu.make_async_remote_copy(
            src_ref=src, dst_ref=dst, send_sem=send_sem, recv_sem=recv_sem,
            device_id=device, device_id_type=MESH,
        )

    A, B = 0, 1

    def index(cx, cy, piece):
        return piece * (NX * NY) + cx * NY + cy

    def m_place(cx, cy, piece):
        return m_all.at[pl.ds(pl.multiple_of((cx * 4 + cy * 2 + c) * rows + piece * half, half), half)]

    def e_place(cx, cy, piece):
        return e_all.at[pl.ds(pl.multiple_of((cx * NY + cy) * rows + piece * half, half), half)]

    def m_to(device, cx, cy, piece, src=None):
        here = m_place(cx, cy, piece)
        recv = m_recv.at[index(cx, cy, piece)]
        copy(here if src is None else src, here, m_send, recv, device).start()

    def m_over(cx, cy, piece, src=None):
        here = m_place(cx, cy, piece)
        copy(here if src is None else src, here, m_send, m_sib, sibling).start()

    def m_step(cx, cy, piece, *devices):
        here = m_place(cx, cy, piece)
        copy(here, here, m_send, m_recv.at[index(cx, cy, piece)], sibling).wait_recv()
        for device in devices:
            m_to(device, cx, cy, piece)
        m_over(cx, cy, piece)

    def e_to(device, cx, cy, piece, src=None):
        here = e_place(cx, cy, piece)
        recv = e_recv.at[index(cx, cy, piece)]
        copy(here if src is None else src, here, e_send, recv, device).start()

    def e_step(cx, cy, piece, *devices):
        here = e_place(cx, cy, piece)
        copy(here, here, e_send, e_recv.at[index(cx, cy, piece)], sibling).wait_recv()
        for device in devices:
            e_to(device, cx, cy, piece)

    def one(step):
        step(xb, y, A, ahead, across)
        step(x, yo, B, ahead, behind)
        step(xa, y, A, across)

    def two(step):
        step(x, yo, A)
        step(xa, y, B, behind)
        step(xb, y, B)

    def h_place(cy, cz):
        return h_all.at[pl.ds(pl.multiple_of((cy * nz + cz) * shard + c * part, part), part)]

    def h_to(device, recv, cy, cz, src=None):
        here = h_place(cy, cz)
        copy(here if src is None else src, here, h_send, recv, device).start()

    def h_got(recv, cy, cz):
        here = h_place(cy, cz)
        copy(here, here, h_send, recv, sibling).wait_recv()

    def h_step(d, *steps):
        cz = zat(d)
        h_got(hz_recv.at[cz], yh, cz)
        for step in steps:
            h_to(along(step), hz_recv.at[cz], yh, cz)
        h_to(partner, hy_recv.at[cz], yh, cz)
        h_to(sibling, h_sib.at[0], yh, cz)

    def crossed(*ds):
        for d in ds:
            cz = zat(d)
            h_got(hy_recv.at[cz], 1 - yh, cz)
            h_to(sibling, h_sib.at[1], 1 - yh, cz)

    h_own = h_ref.at[pl.ds(pl.multiple_of(c * part, part), part)]
    for d in (4, -4, 2, 1, -1):
        h_to(along(d), hz_recv.at[z], yh, z, h_own)
    h_to(partner, hy_recv.at[z], yh, z, h_own)
    m_half = [m_ref.at[pl.ds(piece * half, half)] for piece in (A, B)]
    e_half = [e_ref.at[pl.ds(piece * half, half)] for piece in (A, B)]
    m_to(across, x, y, B, m_half[B])
    m_to(ahead, x, y, A, m_half[A])
    m_to(behind, x, y, A, m_half[A])
    m_to(across, x, y, A, m_half[A])
    m_to(ahead, x, y, B, m_half[B])
    m_to(behind, x, y, B, m_half[B])
    e_to(across, x, y, B, e_half[B])
    m_over(x, y, A, m_half[A])
    m_over(x, y, B, m_half[B])

    h_step(-1)
    h_step(1)
    h_step(-2)
    h_step(-4, 4, 2, 1, -1)
    h_step(4, 2, 1, -1)
    one(m_step)
    e_to(ahead, x, y, A, e_half[A])
    e_to(behind, x, y, A, e_half[A])
    e_to(across, x, y, A, e_half[A])
    e_to(ahead, x, y, B, e_half[B])
    e_to(behind, x, y, B, e_half[B])
    crossed(0)
    for d in (-5, 3, -3, 5, -6, 2):
        h_step(d)
    crossed(-1, 1, -2)
    h_step(8, 2, 1, -1)
    two(m_step)
    crossed(-4, 4)
    m_step(x2, y, A, across)
    m_step(xb, yo, B, ahead)
    m_step(xb, yo, A)
    m_step(xa, yo, A)
    m_step(xa, yo, B)
    one(e_step)
    for d in (7, -7, 6):
        h_step(d)
    crossed(-5, 3, -3, 5, -6, 2, 8)
    two(e_step)
    m_step(x2, y, B)
    m_step(x2, yo, A)
    m_step(x2, yo, B)
    crossed(7, -7, 6)
    for fill in fills:
        fill.wait()

    def all_of(ref, count, send_sem, recv_sem):
        view = ref.at[pl.ds(0, count)]
        return copy(view, view, send_sem, recv_sem, sibling)

    def columns(n):
        return pl.ds(pl.multiple_of(n * CHUNK, CHUNK), CHUNK)

    all_of(h_all, (nz - 1) * part, h_send, h_sib.at[0]).wait_recv()
    all_of(h_all, nz * part, h_send, h_sib.at[1]).wait_recv()

    def p_place(cx, cy, core):
        return p_all.at[pl.ds(pl.multiple_of((cx * 4 + cy * 2 + core) * rows, rows), rows)]

    def project(cx, cy):
        at = pl.ds(pl.multiple_of((cx * NY + cy) * rows, rows), rows)
        to = pl.ds(pl.multiple_of((cx * 4 + cy * 2 + c) * rows, rows), rows)

        @pl.loop(0, width // CHUNK)
        def _(n):
            p_all[to, columns(n)] = jnp.dot(
                e_all[at, :], h_all[:, columns(n)], preferred_element_type=jnp.float32
            ).astype(jnp.bfloat16)

        here = p_place(cx, cy, c)
        copy(here, here, p_send, p_sib.at[cx * NY + cy], sibling).start()

    project(x, y)
    all_of(m_all, group // NC, m_send, m_sib).wait_recv()

    @pl.loop(0, group // CHUNK)
    def _(n):
        at = columns(n)
        scores = scale * lax.dot_general(
            p_all[own, :], m_all[at, :], NT, preferred_element_type=jnp.float32
        )
        st[:, at] = scores
        top = jnp.max(scores, axis=0, keepdims=True)
        lse[rank, :, at] = top + jnp.log(jnp.sum(jnp.exp(scores - top), axis=0, keepdims=True))

    for k in range(1, RANKS):
        copy(lse.at[rank], lse.at[rank], st_send, st_recv.at[rank], peer(k)).start()
    project(x, yo)
    e_step(x2, y, A)
    e_step(xb, yo, B, ahead)
    e_step(xb, yo, A, ahead)
    project(xa, y)
    project(xb, y)
    for k in range(1, RANKS):
        device = peer(k)
        other = device["rep_0"] * 4 + device["rep_1"] * 2 + device["rep_2"]
        copy(lse.at[other], lse.at[other], st_send, st_recv.at[other], sibling).wait_recv()
    parts = lse[...]
    top = jnp.max(parts, axis=0)
    lt[...] = top + jnp.log(jnp.sum(jnp.exp(parts - top[None]), axis=0))

    @pl.loop(0, group // CHUNK)
    def _(n):
        at = columns(n)
        ct[:, at] = jnp.exp(st[:, at] - lt[:, at]).astype(jnp.bfloat16)

    block = st[:, own]
    diagonal = lax.broadcasted_iota(jnp.int32, block.shape, 0) == lax.broadcasted_iota(
        jnp.int32, block.shape, 1
    )
    own_total = lt[:, own]
    loss_ref[...] = own_total - jnp.sum(jnp.where(diagonal, block, 0.0), axis=0, keepdims=True)
    total_rows = jnp.broadcast_to(own_total, (rows, rows)).T[:, :1]

    @pl.loop(0, width // CHUNK)
    def _(n):
        total = jnp.dot(ct[...], m_all[:, columns(n)], preferred_element_type=jnp.float32)
        total = total - m_all[own, columns(n)].astype(jnp.float32)
        dp[:, columns(n)] = (scale * total).astype(jnp.bfloat16)

    e_step(xa, yo, A)
    e_step(xa, yo, B)

    @pl.loop(0, width // CHUNK)
    def _(n):
        grad = lax.dot_general(dp[...], h_all[columns(n), :], NT, preferred_element_type=jnp.float32)
        sg_ref[:, columns(n)] = grad.astype(jnp.bfloat16)
        acc[:, columns(n)] = -p_all[own, columns(n)].astype(jnp.float32)

    def chip(cx, cy):
        here = p_place(cx, cy, co)
        copy(here, here, p_send, p_sib.at[cx * NY + cy], sibling).wait_recv()
        at = pl.ds(pl.multiple_of((cx * 4 + cy * 2) * rows, NC * rows), NC * rows)
        scores = scale * lax.dot_general(
            m_all[own, :], p_all[at, :], NT, preferred_element_type=jnp.float32
        )
        share = jnp.exp(scores - total_rows).astype(jnp.bfloat16)

        @pl.loop(0, width // CHUNK)
        def _(n):
            acc[:, columns(n)] += jnp.dot(
                share, p_all[at, columns(n)], preferred_element_type=jnp.float32
            )

    project(xb, yo)
    chip(x, y)
    project(xa, yo)
    chip(x, yo)
    e_step(x2, y, B)
    project(x2, y)
    chip(xa, y)
    chip(xb, y)
    e_step(x2, yo, A)
    e_step(x2, yo, B)
    project(x2, yo)
    chip(xb, yo)
    chip(xa, yo)
    chip(x2, y)
    chip(x2, yo)

    @pl.loop(0, width // CHUNK)
    def _(n):
        mg_ref[:, columns(n)] = (scale * acc[:, columns(n)]).astype(jnp.bfloat16)

    sent = 6 + 5 + 1 + 2
    all_of(m_all, (sent + 2 * NX * NY) * half, m_send, m_sib).wait_send()
    all_of(e_all, sent * half, e_send, m_sib).wait_send()
    all_of(p_all, NX * NY * rows, p_send, m_sib).wait_send()
    pieces = (6 + 6 + 5 + 5 + 12 * 2) + nz
    all_of(h_all, pieces * part, h_send, m_sib).wait_send()
    view = lse.at[pl.ds(0, RANKS - 1)]
    copy(view, view, st_send, m_sib, sibling).wait_send()


def local(nz, mentions, entity_states, head):
    rows, width = mentions.shape
    group = rows * RANKS
    bf16, f32 = jnp.bfloat16, jnp.float32
    pieces = 2 * NX * NY
    dma = pltpu.SemaphoreType.DMA
    any_spec = pl.BlockSpec(memory_space=pl.ANY)
    vmem_spec = pl.BlockSpec(memory_space=pltpu.VMEM)
    loss, mention_grad, state_grad = pl.pallas_call(
        functools.partial(kernel, nz, 3.0 / math.sqrt(width)),
        out_shape=(
            pltpu.VMEM((1, rows), f32),
            pltpu.VMEM((rows, width), bf16),
            pltpu.VMEM((rows, width), bf16),
        ),
        in_specs=[any_spec] * 3,
        out_specs=(vmem_spec,) * 3,
        scratch_shapes=[
            pltpu.VMEM((group, width), bf16),
            pltpu.VMEM((group // NC, width), bf16),
            pltpu.VMEM((group, width), bf16),
            pltpu.VMEM((width, width), bf16),
            pltpu.VMEM((rows, width), f32),
            pltpu.VMEM((rows, group), f32),
            pltpu.VMEM((rows, group), bf16),
            pltpu.VMEM((RANKS, 1, group), f32),
            pltpu.VMEM((1, group), f32),
            pltpu.VMEM((rows, width), bf16),
            dma((3,)),
            dma((pieces,)),
            dma,
            dma((pieces,)),
            dma((NX * NY,)),
            dma((nz,)),
            dma((nz,)),
            dma((2,)),
            dma((RANKS,)),
            dma, dma, dma, dma, dma,
        ],
        compiler_params=pltpu.CompilerParams(collective_id=0, has_side_effects=True),
    )(mentions, entity_states, head)
    return loss.reshape(rows), mention_grad, state_grad


def solution(mesh):
    torus = Mesh(mesh.devices.reshape(2, 16, 4, 2, 2), DP_REP)
    in_specs = (P(DP_REP, None), P(DP_REP, None), P(("dp_0", "dp_1"), None))
    out_specs = (P(DP_REP), P(DP_REP, None), P(DP_REP, None))
    return jax.shard_map(
        functools.partial(local, 16), mesh=torus, in_specs=in_specs, out_specs=out_specs, check_vma=False
    )
```

```python
import functools
import math

import jax
import jax.numpy as jnp
from jax import lax
from jax.experimental import pallas as pl
from jax.experimental.pallas import tpu as pltpu
from jax.sharding import Mesh
from jax.sharding import PartitionSpec as P

DP_REP = ("dp_0", "dp_1", "rep_0", "rep_1", "rep_2")
MESH = pl.DeviceIdType.MESH
NX, NY, NC = 4, 2, 2
RANKS = NX * NY * NC
CHUNK = 256
WIDE = 512
BITS = 2
NT = (((1,), (1,)), ((), ()))


def kernel(
    nz, scale,
    m_ref, e_ref, h_ref,
    loss_ref, mg_ref, sg_ref,
    m_all, e_all, p_all, h_all, st, ct, lse, lt, dp,
    local_sem, m_recv, m_sib, e_recv, e_sib, p_sib, hz_recv, hy_recv, h_sib, st_recv,
    m_send, e_send, p_send, h_send, st_send, ready,
):
    rows, width = m_ref.shape
    shard = h_ref.shape[0]
    bit = rows // BITS
    group = rows * RANKS
    yh, z = lax.axis_index("dp_0"), lax.axis_index("dp_1")
    x, y, c = lax.axis_index("rep_0"), lax.axis_index("rep_1"), lax.axis_index("rep_2")
    xa, xb, x2 = lax.rem(x + 1, NX), lax.rem(x + 3, NX), lax.rem(x + 2, NX)
    yo, co = 1 - y, 1 - c
    rank = x * 4 + y * 2 + c
    across, sibling = {"rep_1": yo}, {"rep_2": co}
    plus, minus = {"rep_0": xa}, {"rep_0": xb}
    head, bulk = c == 0, c == 1

    def zat(d):
        return lax.rem(z + nz + d, nz)

    def along(d):
        return {"dp_1": zat(d)}

    def beyond(d):
        return {"dp_0": 1 - yh, "rep_1": yo, "dp_1": zat(d)}

    def peer(k):
        return {
            "rep_0": lax.rem(x + k // 4, NX),
            "rep_1": lax.rem(y + (k // 2) % 2, NY),
            "rep_2": lax.rem(c + k % 2, NC),
        }

    def signal(sem, device):
        pl.semaphore_signal(sem, inc=1, device_id=device, device_id_type=MESH)

    barrier = pltpu.get_barrier_semaphore()
    for k in range(1, RANKS):
        signal(barrier, peer(k))

    @pl.when(head)
    def _():
        for device in [along(-3), along(-2), along(-1), beyond(0), beyond(-1), beyond(-2)]:
            signal(barrier, device)

    own = pl.ds(pl.multiple_of(rank * rows, rows), rows)
    own_shard = pl.ds(pl.multiple_of((yh * nz + z) * shard, shard), shard)
    fills = [
        pltpu.make_async_copy(m_ref, m_all.at[own], local_sem.at[0]),
        pltpu.make_async_copy(e_ref, e_all.at[own], local_sem.at[1]),
        pltpu.make_async_copy(h_ref, h_all.at[own_shard], local_sem.at[2]),
    ]
    for fill in fills:
        fill.start()

    def copy(src, dst, send_sem, recv_sem, device):
        return pltpu.make_async_remote_copy(
            src_ref=src, dst_ref=dst, send_sem=send_sem, recv_sem=recv_sem,
            device_id=device, device_id_type=MESH,
        )

    A, B = 0, 1

    def chip(cx, cy):
        return cx * NY + cy

    def index(cx, cy, piece):
        return piece * (NX * NY) + chip(cx, cy)

    def place(array, cx, cy, piece):
        return array.at[pl.ds(pl.multiple_of((cx * 4 + cy * 2 + piece) * rows, rows), rows)]

    def bulk_of(array, send_sem, recv, over, ahead, behind, xa, xb):
        def here(cx, cy, piece, k):
            return place(array, cx, cy, piece).at[pl.ds(k * bit, bit)]

        def to(device, cx, cy, piece, k, src=None):
            at = here(cx, cy, piece, k)
            recv_sem = recv.at[index(cx, cy, piece) * BITS + k]
            copy(at if src is None else src.at[pl.ds(k * bit, bit)], at, send_sem, recv_sem, device).start()

        def got(cx, cy, piece, k):
            at = here(cx, cy, piece, k)
            copy(at, at, send_sem, recv.at[index(cx, cy, piece) * BITS + k], sibling).wait_recv()

        def step(cx, cy, piece, *devices):
            for k in range(BITS):
                got(cx, cy, piece, k)
                for device in devices:
                    to(device, cx, cy, piece, k)
                over(here(cx, cy, piece, k), cx, cy, piece)

        def start(source):
            for k in range(BITS):
                for device in (across, ahead, behind):
                    to(device, x, y, B, k, source)
            for k in range(BITS):
                got(x, y, A, k)
                for device in (ahead, behind, across):
                    to(device, x, y, A, k)

        def one():
            step(x, yo, B, ahead, behind)
            step(xa, y, B, behind)
            step(xb, y, B)
            step(xb, y, A, ahead, across)

        def two():
            step(xa, y, A, across)
            step(x, yo, A)
            step(xb, yo, B, ahead)
            step(xa, yo, B)

        def three():
            step(x2, y, B)
            step(x2, y, A, across)
            step(xb, yo, A)
            step(xa, yo, A)

        def four():
            step(x2, yo, B)
            step(x2, yo, A)

        return start, one, two, three, four

    def m_over(here, cx, cy, piece):
        copy(here, here, m_send, m_sib, sibling).start()

    def e_over(here, cx, cy, piece):
        if piece == A:
            copy(here, here, e_send, e_sib.at[chip(cx, cy)], sibling).start()

    def wait_sent(ref, sem, total):
        most = ref.shape[0]
        while total > 0:
            view = ref.at[pl.ds(0, min(total, most))]
            copy(view, view, sem, m_sib, sibling).wait_send()
            total -= most

    def wait_got(ref, sem, total):
        view = ref.at[pl.ds(0, total)]
        copy(view, view, m_send, sem, sibling).wait_recv()

    @pl.when(bulk)
    def _():
        pl.semaphore_wait(barrier, RANKS - 1)
        m_start, m_one, m_two, m_three, m_four = bulk_of(
            m_all, m_send, m_recv, m_over, plus, minus, xa, xb
        )
        e_start, e_one, e_two, e_three, e_four = bulk_of(
            e_all, e_send, e_recv, e_over, minus, plus, xb, xa
        )
        m_start(m_ref)
        copy(m_ref, place(m_all, x, y, B), m_send, m_sib, sibling).start()
        m_one()
        e_start(e_ref)
        m_two()
        m_three()
        e_one()
        m_four()
        e_two()
        e_three()
        e_four()

    def h_place(cy, cz):
        return h_all.at[pl.ds(pl.multiple_of((cy * nz + cz) * shard, shard), shard)]

    def h_to(device, recv, cy, cz, src=None):
        here = h_place(cy, cz)
        copy(here if src is None else src, here, h_send, recv.at[cz] if device is not sibling else recv, device).start()

    def h_got(recv, cy, d):
        here = h_place(cy, zat(d))
        copy(here, here, h_send, recv.at[zat(d)], sibling).wait_recv()

    def h_line(d, jumps, near):
        h_got(hz_recv, yh, d)
        cz = zat(d)
        for step in jumps:
            h_to(along(step), hz_recv, yh, cz)
        for step in near:
            h_to(along(step), hz_recv, yh, cz)
            h_to(beyond(step), hy_recv, yh, cz)
        h_to(beyond(0), hy_recv, yh, cz)
        h_to(sibling, h_sib, yh, cz)

    def h_leaf(*ds):
        for d in ds:
            h_got(hz_recv, yh, d)
            h_to(sibling, h_sib, yh, zat(d))

    def crossed(*ds):
        for d in ds:
            h_got(hy_recv, 1 - yh, d)
            h_to(sibling, h_sib, 1 - yh, zat(d))

    def give(source, array, send_sem, recv):
        for k in range(BITS):
            at = pl.ds(k * bit, bit)
            recv_sem = recv.at[index(x, y, A) * BITS + k]
            copy(source.at[at], place(array, x, y, A).at[at], send_sem, recv_sem, sibling).start()

    @pl.when(head)
    def _():
        pl.semaphore_wait(barrier, RANKS + 5)
        for device in [along(3), along(1), beyond(1)]:
            signal(ready, device)
        give(m_ref, m_all, m_send, m_recv)
        h_to(along(3), hz_recv, yh, z, h_ref)
        h_to(along(1), hz_recv, yh, z, h_ref)
        h_to(beyond(1), hy_recv, yh, z, h_ref)
        h_to(beyond(0), hy_recv, yh, z, h_ref)
        give(e_ref, e_all, e_send, e_recv)
        pl.semaphore_wait(ready, 3)
        h_to(along(-3), hz_recv, yh, z, h_ref)
        h_to(along(-1), hz_recv, yh, z, h_ref)
        h_to(beyond(-1), hy_recv, yh, z, h_ref)
        h_leaf(-1)
        h_line(-3, (3,), (1, -1))
        h_leaf(1)
        h_line(3, (-3,), (1, -1))
        crossed(0, -1, 1)
        h_leaf(-4, 2, 4, -2)
        h_line(-6, (), (2, 1, -1))
        crossed(-3, 3)
        h_line(6, (), (1, -1))
        crossed(-4, 2, 4, -2)
        h_leaf(-7, 5, 7, -5, 8)
        crossed(-6, 6, -7, 5, 7, -5, 8)

    for fill in fills:
        fill.wait()

    @pl.when(bulk)
    def _():
        wait_got(h_all, h_sib, (2 * nz - 1) * shard)

    def columns(n, size=CHUNK):
        return pl.ds(pl.multiple_of(n * size, size), size)

    def project(*chips):
        at = [pl.ds(pl.multiple_of((cx * 4 + cy * 2 + c) * rows, rows), rows) for cx, cy in chips]

        @pl.loop(0, width // CHUNK)
        def _(n):
            for block in at:
                p_all[block, columns(n)] = jnp.dot(
                    e_all[block, :], h_all[:, columns(n)], preferred_element_type=jnp.float32
                ).astype(jnp.bfloat16)

        for cx, cy in chips:
            here = place(p_all, cx, cy, c)
            copy(here, here, p_send, p_sib.at[chip(cx, cy)], sibling).start()

    project((x, y))

    @pl.when(head)
    def _():
        wait_got(m_all, m_sib, (RANKS - 1) * rows)

    @pl.loop(0, group // WIDE)
    def _(n):
        at = columns(n, WIDE)
        scores = scale * lax.dot_general(
            m_all[at, :], p_all[own, :], NT, preferred_element_type=jnp.float32
        ).T
        st[:, at] = scores
        top = jnp.max(scores, axis=0, keepdims=True)
        lse[rank, :, at] = top + jnp.log(jnp.sum(jnp.exp(scores - top), axis=0, keepdims=True))

    for k in range(1, RANKS):
        copy(lse.at[rank], lse.at[rank], st_send, st_recv.at[rank], peer(k)).start()

    others = [(x, yo), (xa, y), (xb, y), (x2, y), (xa, yo), (xb, yo), (x2, yo)]

    @pl.when(head)
    def _():
        for cx, cy in others:
            here = place(e_all, cx, cy, A)
            copy(here, here, e_send, e_sib.at[chip(cx, cy)], sibling).wait_recv()

    project(*others)
    for k in range(1, RANKS):
        device = peer(k)
        other = device["rep_0"] * 4 + device["rep_1"] * 2 + device["rep_2"]
        copy(lse.at[other], lse.at[other], st_send, st_recv.at[other], sibling).wait_recv()
    parts = lse[...]
    top = jnp.max(parts, axis=0)
    lt[...] = top + jnp.log(jnp.sum(jnp.exp(parts - top[None]), axis=0))

    @pl.loop(0, group // CHUNK)
    def _(n):
        at = columns(n)
        ct[:, at] = jnp.exp(st[:, at] - lt[:, at]).astype(jnp.bfloat16)

    block = st[:, own]
    diagonal = lax.broadcasted_iota(jnp.int32, block.shape, 0) == lax.broadcasted_iota(
        jnp.int32, block.shape, 1
    )
    own_total = lt[:, own]
    loss_ref[...] = own_total - jnp.sum(jnp.where(diagonal, block, 0.0), axis=0, keepdims=True)
    total_rows = jnp.broadcast_to(own_total, (rows, rows)).T[:, :1]

    @pl.loop(0, width // CHUNK)
    def _(n):
        total = jnp.dot(ct[...], m_all[:, columns(n)], preferred_element_type=jnp.float32)
        total = total - m_all[own, columns(n)].astype(jnp.float32)
        dp[:, columns(n)] = (scale * total).astype(jnp.bfloat16)

    @pl.loop(0, width // WIDE)
    def _(n):
        at = columns(n, WIDE)
        grad = lax.dot_general(h_all[at, :], dp[...], NT, preferred_element_type=jnp.float32)
        sg_ref[:, at] = grad.T.astype(jnp.bfloat16)

    for cx, cy in [(x, y)] + others:
        here = place(p_all, cx, cy, co)
        copy(here, here, p_send, p_sib.at[chip(cx, cy)], sibling).wait_recv()

    @pl.loop(0, group // WIDE)
    def _(n):
        at = columns(n, WIDE)
        scores = scale * lax.dot_general(
            p_all[at, :], m_all[own, :], NT, preferred_element_type=jnp.float32
        ).T
        ct[:, at] = jnp.exp(scores - total_rows).astype(jnp.bfloat16)

    @pl.loop(0, width // CHUNK)
    def _(n):
        total = jnp.dot(ct[...], p_all[:, columns(n)], preferred_element_type=jnp.float32)
        total = total - p_all[own, columns(n)].astype(jnp.float32)
        mg_ref[:, columns(n)] = (scale * total).astype(jnp.bfloat16)

    moves = 6 + 4 + 2 + 1 + 1

    @pl.when(bulk)
    def _():
        wait_sent(m_all, m_send, (moves + RANKS - 1) * rows)
        wait_sent(e_all, e_send, (moves + NX * NY - 1) * rows)

    @pl.when(head)
    def _():
        wait_sent(m_all, m_send, rows)
        wait_sent(e_all, e_send, rows)
        wait_sent(h_all, h_send, (7 + 7 + 7 + 8 + 6 + 11 + nz) * shard)

    wait_sent(p_all, p_send, NX * NY * rows)
    view = lse.at[pl.ds(0, RANKS - 1)]
    copy(view, view, st_send, m_sib, sibling).wait_send()


def local(nz, mentions, entity_states, head):
    rows, width = mentions.shape
    group = rows * RANKS
    bf16, f32 = jnp.bfloat16, jnp.float32
    pieces = 2 * NX * NY
    dma = pltpu.SemaphoreType.DMA
    any_spec = pl.BlockSpec(memory_space=pl.ANY)
    vmem_spec = pl.BlockSpec(memory_space=pltpu.VMEM)
    loss, mention_grad, state_grad = pl.pallas_call(
        functools.partial(kernel, nz, 3.0 / math.sqrt(width)),
        out_shape=(
            pltpu.VMEM((1, rows), f32),
            pltpu.VMEM((rows, width), bf16),
            pltpu.VMEM((rows, width), bf16),
        ),
        in_specs=[any_spec] * 3,
        out_specs=(vmem_spec,) * 3,
        scratch_shapes=[
            pltpu.VMEM((group, width), bf16),
            pltpu.VMEM((group, width), bf16),
            pltpu.VMEM((group, width), bf16),
            pltpu.VMEM((width, width), bf16),
            pltpu.VMEM((rows, group), f32),
            pltpu.VMEM((rows, group), bf16),
            pltpu.VMEM((RANKS, 1, group), f32),
            pltpu.VMEM((1, group), f32),
            pltpu.VMEM((rows, width), bf16),
            dma((3,)),
            dma((pieces * BITS,)),
            dma,
            dma((pieces * BITS,)),
            dma((NX * NY,)),
            dma((NX * NY,)),
            dma((nz,)),
            dma((nz,)),
            dma,
            dma((RANKS,)),
            dma, dma, dma, dma, dma,
            pltpu.SemaphoreType.REGULAR,
        ],
        compiler_params=pltpu.CompilerParams(collective_id=0, has_side_effects=True),
    )(mentions, entity_states, head)
    return loss.reshape(rows), mention_grad, state_grad


def solution(mesh):
    torus = Mesh(mesh.devices.reshape(2, 16, 4, 2, 2), DP_REP)
    in_specs = (P(DP_REP, None), P(DP_REP, None), P(("dp_0", "dp_1"), None))
    out_specs = (P(DP_REP), P(DP_REP, None), P(DP_REP, None))
    return jax.shard_map(
        functools.partial(local, 16), mesh=torus, in_specs=in_specs, out_specs=out_specs, check_vma=False
    )
```

```python
import functools
import math

import jax
import jax.numpy as jnp
from jax import lax
from jax.experimental import pallas as pl
from jax.experimental.pallas import tpu as pltpu
from jax.sharding import Mesh
from jax.sharding import PartitionSpec as P

DP_REP = ("dp_0", "dp_1", "rep_0", "rep_1", "rep_2")
MESH = pl.DeviceIdType.MESH
NX, NY, NC = 4, 2, 2
RANKS = NX * NY * NC
CHUNK = 256
WIDE = 512
BITS = 2
NT = (((1,), (1,)), ((), ()))


def kernel(
    nz, scale,
    m_ref, e_ref, h_ref,
    loss_ref, mg_ref, sg_ref,
    m_all, e_all, p_all, h_all, st, ct, lse, lt, dp,
    local_sem, m_recv, m_sib, e_recv, e_sib, p_sib, hz_recv, hy_recv, h_sib, st_recv,
    m_send, e_send, p_send, h_send, st_send, ready,
):
    rows, width = m_ref.shape
    shard = h_ref.shape[0]
    bit = rows // BITS
    group = rows * RANKS
    yh, z = lax.axis_index("dp_0"), lax.axis_index("dp_1")
    x, y, c = lax.axis_index("rep_0"), lax.axis_index("rep_1"), lax.axis_index("rep_2")
    xa, xb, x2 = lax.rem(x + 1, NX), lax.rem(x + 3, NX), lax.rem(x + 2, NX)
    yo, co = 1 - y, 1 - c
    rank = x * 4 + y * 2 + c
    across, sibling = {"rep_1": yo}, {"rep_2": co}
    plus, minus = {"rep_0": xa}, {"rep_0": xb}
    head, bulk = c == 0, c == 1

    def zat(d):
        return lax.rem(z + nz + d, nz)

    def along(d):
        return {"dp_1": zat(d)}

    def beyond(d):
        return {"dp_0": 1 - yh, "rep_1": yo, "dp_1": zat(d)}

    def peer(k):
        return {
            "rep_0": lax.rem(x + k // 4, NX),
            "rep_1": lax.rem(y + (k // 2) % 2, NY),
            "rep_2": lax.rem(c + k % 2, NC),
        }

    def signal(sem, device):
        pl.semaphore_signal(sem, inc=1, device_id=device, device_id_type=MESH)

    barrier = pltpu.get_barrier_semaphore()
    for k in range(1, RANKS):
        signal(barrier, peer(k))

    @pl.when(head)
    def _():
        for device in [along(-3), along(-2), along(-1), beyond(0), beyond(-1), beyond(-2)]:
            signal(barrier, device)

    own = pl.ds(pl.multiple_of(rank * rows, rows), rows)
    own_shard = pl.ds(pl.multiple_of((yh * nz + z) * shard, shard), shard)
    fills = [
        pltpu.make_async_copy(m_ref, m_all.at[own], local_sem.at[0]),
        pltpu.make_async_copy(e_ref, e_all.at[own], local_sem.at[1]),
        pltpu.make_async_copy(h_ref, h_all.at[own_shard], local_sem.at[2]),
    ]
    for fill in fills:
        fill.start()

    def copy(src, dst, send_sem, recv_sem, device):
        return pltpu.make_async_remote_copy(
            src_ref=src, dst_ref=dst, send_sem=send_sem, recv_sem=recv_sem,
            device_id=device, device_id_type=MESH,
        )

    A, B = 0, 1

    def chip(cx, cy):
        return cx * NY + cy

    def index(cx, cy, piece):
        return piece * (NX * NY) + chip(cx, cy)

    def place(array, cx, cy, piece):
        return array.at[pl.ds(pl.multiple_of((cx * 4 + cy * 2 + piece) * rows, rows), rows)]

    def bulk_of(array, send_sem, recv, over, ahead, behind, xa, xb, turn):
        def here(cx, cy, piece, k):
            return place(array, cx, cy, piece).at[pl.ds(k * bit, bit)]

        def to(device, cx, cy, piece, k, src=None):
            at = here(cx, cy, piece, k)
            recv_sem = recv.at[index(cx, cy, piece) * BITS + k]
            copy(at if src is None else src.at[pl.ds(k * bit, bit)], at, send_sem, recv_sem, device).start()

        def got(cx, cy, piece, k):
            at = here(cx, cy, piece, k)
            copy(at, at, send_sem, recv.at[index(cx, cy, piece) * BITS + k], sibling).wait_recv()

        def step(cx, cy, piece, *devices):
            for k in range(BITS):
                got(cx, cy, piece, k)
                for device in devices:
                    to(device, cx, cy, piece, k)
                over(here(cx, cy, piece, k), cx, cy, piece)

        def first(source):
            for k in range(BITS):
                to(across, x, y, B, k, source)

        def start(source):
            for k in range(BITS):
                for device in (ahead, behind):
                    to(device, x, y, B, k, source)
            for k in range(BITS):
                got(x, y, A, k)
                for device in (ahead, behind, across):
                    to(device, x, y, A, k)

        def one():
            step(x, yo, B, ahead, behind)
            step(xa, y, B, behind)
            step(xb, y, B)
            step(xb, y, A, ahead, across)

        def two():
            step(xa, y, A, across)
            step(x, yo, A)
            step(xb, yo, B, ahead)
            step(xa, yo, B)

        def three():
            step(x2, y, B)
            step(x2, y, A, *(() if turn else (across,)))
            step(xb, yo, A, *((ahead,) if turn else ()))
            step(xa, yo, A)

        def four():
            step(x2, yo, B)
            step(x2, yo, A)

        return first, start, one, two, three, four

    def m_over(here, cx, cy, piece):
        copy(here, here, m_send, m_sib, sibling).start()

    def e_over(here, cx, cy, piece):
        if piece == A:
            copy(here, here, e_send, e_sib.at[chip(cx, cy)], sibling).start()

    def wait_sent(ref, sem, total):
        most = ref.shape[0]
        while total > 0:
            view = ref.at[pl.ds(0, min(total, most))]
            copy(view, view, sem, m_sib, sibling).wait_send()
            total -= most

    def wait_got(ref, sem, total):
        view = ref.at[pl.ds(0, total)]
        copy(view, view, m_send, sem, sibling).wait_recv()

    m_first, m_start, m_one, m_two, m_three, m_four = bulk_of(
        m_all, m_send, m_recv, m_over, plus, minus, xa, xb, False
    )
    e_first, e_start, e_one, e_two, e_three, e_four = bulk_of(
        e_all, e_send, e_recv, e_over, minus, plus, xb, xa, True
    )

    @pl.when(bulk)
    def _():
        pl.semaphore_wait(barrier, RANKS - 1)
        m_first(m_ref)
        m_start(m_ref)
        e_first(e_ref)
        e_start(e_ref)
        copy(m_ref, place(m_all, x, y, B), m_send, m_sib, sibling).start()
        m_one()
        e_one()
        m_two()
        e_two()
        m_three()
        e_three()
        m_four()
        e_four()

    def h_place(cy, cz):
        return h_all.at[pl.ds(pl.multiple_of((cy * nz + cz) * shard, shard), shard)]

    def h_to(device, recv, cy, cz, src=None):
        here = h_place(cy, cz)
        copy(here if src is None else src, here, h_send, recv.at[cz] if device is not sibling else recv, device).start()

    def h_got(recv, cy, d):
        here = h_place(cy, zat(d))
        copy(here, here, h_send, recv.at[zat(d)], sibling).wait_recv()

    def h_line(d, jumps, near):
        h_got(hz_recv, yh, d)
        cz = zat(d)
        for step in jumps:
            h_to(along(step), hz_recv, yh, cz)
        for step in near:
            h_to(along(step), hz_recv, yh, cz)
            h_to(beyond(step), hy_recv, yh, cz)
        h_to(beyond(0), hy_recv, yh, cz)
        h_to(sibling, h_sib, yh, cz)

    def h_leaf(*ds):
        for d in ds:
            h_got(hz_recv, yh, d)
            h_to(sibling, h_sib, yh, zat(d))

    def crossed(*ds):
        for d in ds:
            h_got(hy_recv, 1 - yh, d)
            h_to(sibling, h_sib, 1 - yh, zat(d))

    def give(source, array, send_sem, recv):
        for k in range(BITS):
            at = pl.ds(k * bit, bit)
            recv_sem = recv.at[index(x, y, A) * BITS + k]
            copy(source.at[at], place(array, x, y, A).at[at], send_sem, recv_sem, sibling).start()

    @pl.when(head)
    def _():
        pl.semaphore_wait(barrier, RANKS + 5)
        for device in [along(3), along(1), beyond(1)]:
            signal(ready, device)
        give(m_ref, m_all, m_send, m_recv)
        h_to(along(3), hz_recv, yh, z, h_ref)
        h_to(along(1), hz_recv, yh, z, h_ref)
        h_to(beyond(1), hy_recv, yh, z, h_ref)
        h_to(beyond(0), hy_recv, yh, z, h_ref)
        give(e_ref, e_all, e_send, e_recv)
        pl.semaphore_wait(ready, 3)
        h_to(along(-3), hz_recv, yh, z, h_ref)
        h_to(along(-1), hz_recv, yh, z, h_ref)
        h_to(beyond(-1), hy_recv, yh, z, h_ref)
        h_leaf(-1)
        h_line(-3, (3,), (1, -1))
        h_leaf(1)
        h_line(3, (-3,), (1, -1))
        crossed(0, -1, 1)
        h_leaf(-4, 2, 4, -2)
        h_line(-6, (), (2, 1, -1))
        crossed(-3, 3)
        h_line(6, (), (1, -1))
        crossed(-4, 2, 4, -2)
        h_leaf(-7, 5, 7, -5, 8)
        crossed(-6, 6, -7, 5, 7, -5, 8)

    for fill in fills:
        fill.wait()

    @pl.when(bulk)
    def _():
        wait_got(h_all, h_sib, (2 * nz - 1) * shard)

    def columns(n, size=CHUNK):
        return pl.ds(pl.multiple_of(n * size, size), size)

    def project(*chips):
        at = [pl.ds(pl.multiple_of((cx * 4 + cy * 2 + c) * rows, rows), rows) for cx, cy in chips]

        @pl.loop(0, width // CHUNK)
        def _(n):
            for block in at:
                p_all[block, columns(n)] = jnp.dot(
                    e_all[block, :], h_all[:, columns(n)], preferred_element_type=jnp.float32
                ).astype(jnp.bfloat16)

        for cx, cy in chips:
            here = place(p_all, cx, cy, c)
            copy(here, here, p_send, p_sib.at[chip(cx, cy)], sibling).start()

    project((x, y))

    @pl.when(head)
    def _():
        wait_got(m_all, m_sib, (RANKS - 1) * rows)

    @pl.loop(0, group // WIDE)
    def _(n):
        at = columns(n, WIDE)
        scores = scale * lax.dot_general(
            m_all[at, :], p_all[own, :], NT, preferred_element_type=jnp.float32
        ).T
        st[:, at] = scores
        top = jnp.max(scores, axis=0, keepdims=True)
        lse[rank, :, at] = top + jnp.log(jnp.sum(jnp.exp(scores - top), axis=0, keepdims=True))

    for k in range(1, RANKS):
        copy(lse.at[rank], lse.at[rank], st_send, st_recv.at[rank], peer(k)).start()

    others = [(x, yo), (xa, y), (xb, y), (x2, y), (xa, yo), (xb, yo), (x2, yo)]

    @pl.when(head)
    def _():
        for cx, cy in others:
            here = place(e_all, cx, cy, A)
            copy(here, here, e_send, e_sib.at[chip(cx, cy)], sibling).wait_recv()

    project(*others)
    for k in range(1, RANKS):
        device = peer(k)
        other = device["rep_0"] * 4 + device["rep_1"] * 2 + device["rep_2"]
        copy(lse.at[other], lse.at[other], st_send, st_recv.at[other], sibling).wait_recv()
    parts = lse[...]
    top = jnp.max(parts, axis=0)
    lt[...] = top + jnp.log(jnp.sum(jnp.exp(parts - top[None]), axis=0))

    @pl.loop(0, group // CHUNK)
    def _(n):
        at = columns(n)
        ct[:, at] = jnp.exp(st[:, at] - lt[:, at]).astype(jnp.bfloat16)

    block = st[:, own]
    diagonal = lax.broadcasted_iota(jnp.int32, block.shape, 0) == lax.broadcasted_iota(
        jnp.int32, block.shape, 1
    )
    own_total = lt[:, own]
    loss_ref[...] = own_total - jnp.sum(jnp.where(diagonal, block, 0.0), axis=0, keepdims=True)
    total_rows = jnp.broadcast_to(own_total, (rows, rows)).T[:, :1]

    @pl.loop(0, width // CHUNK)
    def _(n):
        total = jnp.dot(ct[...], m_all[:, columns(n)], preferred_element_type=jnp.float32)
        total = total - m_all[own, columns(n)].astype(jnp.float32)
        dp[:, columns(n)] = (scale * total).astype(jnp.bfloat16)

    @pl.loop(0, width // WIDE)
    def _(n):
        at = columns(n, WIDE)
        grad = lax.dot_general(h_all[at, :], dp[...], NT, preferred_element_type=jnp.float32)
        sg_ref[:, at] = grad.T.astype(jnp.bfloat16)

    for cx, cy in [(x, y)] + others:
        here = place(p_all, cx, cy, co)
        copy(here, here, p_send, p_sib.at[chip(cx, cy)], sibling).wait_recv()

    @pl.loop(0, group // WIDE)
    def _(n):
        at = columns(n, WIDE)
        scores = scale * lax.dot_general(
            p_all[at, :], m_all[own, :], NT, preferred_element_type=jnp.float32
        ).T
        ct[:, at] = jnp.exp(scores - total_rows).astype(jnp.bfloat16)

    @pl.loop(0, width // CHUNK)
    def _(n):
        total = jnp.dot(ct[...], p_all[:, columns(n)], preferred_element_type=jnp.float32)
        total = total - p_all[own, columns(n)].astype(jnp.float32)
        mg_ref[:, columns(n)] = (scale * total).astype(jnp.bfloat16)

    moves = 6 + 4 + 2 + 1 + 1

    @pl.when(bulk)
    def _():
        wait_sent(m_all, m_send, (moves + RANKS - 1) * rows)
        wait_sent(e_all, e_send, (moves + NX * NY - 1) * rows)

    @pl.when(head)
    def _():
        wait_sent(m_all, m_send, rows)
        wait_sent(e_all, e_send, rows)
        wait_sent(h_all, h_send, (7 + 7 + 7 + 8 + 6 + 11 + nz) * shard)

    wait_sent(p_all, p_send, NX * NY * rows)
    view = lse.at[pl.ds(0, RANKS - 1)]
    copy(view, view, st_send, m_sib, sibling).wait_send()


def local(nz, mentions, entity_states, head):
    rows, width = mentions.shape
    group = rows * RANKS
    bf16, f32 = jnp.bfloat16, jnp.float32
    pieces = 2 * NX * NY
    dma = pltpu.SemaphoreType.DMA
    any_spec = pl.BlockSpec(memory_space=pl.ANY)
    vmem_spec = pl.BlockSpec(memory_space=pltpu.VMEM)
    loss, mention_grad, state_grad = pl.pallas_call(
        functools.partial(kernel, nz, 3.0 / math.sqrt(width)),
        out_shape=(
            pltpu.VMEM((1, rows), f32),
            pltpu.VMEM((rows, width), bf16),
            pltpu.VMEM((rows, width), bf16),
        ),
        in_specs=[any_spec] * 3,
        out_specs=(vmem_spec,) * 3,
        scratch_shapes=[
            pltpu.VMEM((group, width), bf16),
            pltpu.VMEM((group, width), bf16),
            pltpu.VMEM((group, width), bf16),
            pltpu.VMEM((width, width), bf16),
            pltpu.VMEM((rows, group), f32),
            pltpu.VMEM((rows, group), bf16),
            pltpu.VMEM((RANKS, 1, group), f32),
            pltpu.VMEM((1, group), f32),
            pltpu.VMEM((rows, width), bf16),
            dma((3,)),
            dma((pieces * BITS,)),
            dma,
            dma((pieces * BITS,)),
            dma((NX * NY,)),
            dma((NX * NY,)),
            dma((nz,)),
            dma((nz,)),
            dma,
            dma((RANKS,)),
            dma, dma, dma, dma, dma,
            pltpu.SemaphoreType.REGULAR,
        ],
        compiler_params=pltpu.CompilerParams(collective_id=0, has_side_effects=True),
    )(mentions, entity_states, head)
    return loss.reshape(rows), mention_grad, state_grad


def solution(mesh):
    torus = Mesh(mesh.devices.reshape(2, 16, 4, 2, 2), DP_REP)
    in_specs = (P(DP_REP, None), P(DP_REP, None), P(("dp_0", "dp_1"), None))
    out_specs = (P(DP_REP), P(DP_REP, None), P(DP_REP, None))
    return jax.shard_map(
        functools.partial(local, 16), mesh=torus, in_specs=in_specs, out_specs=out_specs, check_vma=False
    )
```

```python
import functools
import math

import jax
import jax.numpy as jnp
from jax import lax
from jax.experimental import pallas as pl
from jax.experimental.pallas import tpu as pltpu
from jax.sharding import Mesh
from jax.sharding import PartitionSpec as P

DP_REP = ("dp_0", "dp_1", "rep_0", "rep_1", "rep_2")
MESH = pl.DeviceIdType.MESH
NX, NY, NC = 4, 2, 2
RANKS = NX * NY * NC
CHUNK = 512
WIDE = 512
BITS = 2
NT = (((1,), (1,)), ((), ()))


def kernel(
    nz, scale,
    m_ref, e_ref, h_ref,
    loss_ref, mg_ref, sg_ref,
    m_all, e_all, p_all, h_all, st, ct, lse, lt, dp,
    local_sem, m_recv, m_sib, e_recv, e_sib, p_sib, hz_recv, hy_recv, h_sib, st_recv,
    m_send, e_send, p_send, h_send, st_send, ready,
):
    rows, width = m_ref.shape
    shard = h_ref.shape[0]
    bit = rows // BITS
    group = rows * RANKS
    yh, z = lax.axis_index("dp_0"), lax.axis_index("dp_1")
    x, y, c = lax.axis_index("rep_0"), lax.axis_index("rep_1"), lax.axis_index("rep_2")
    xa, xb, x2 = lax.rem(x + 1, NX), lax.rem(x + 3, NX), lax.rem(x + 2, NX)
    yo, co = 1 - y, 1 - c
    rank = x * 4 + y * 2 + c
    across, sibling = {"rep_1": yo}, {"rep_2": co}
    plus, minus = {"rep_0": xa}, {"rep_0": xb}
    head, bulk = c == 0, c == 1

    def zat(d):
        return lax.rem(z + nz + d, nz)

    def along(d):
        return {"dp_1": zat(d)}

    def beyond(d):
        return {"dp_0": 1 - yh, "rep_1": yo, "dp_1": zat(d)}

    def peer(k):
        return {
            "rep_0": lax.rem(x + k // 4, NX),
            "rep_1": lax.rem(y + (k // 2) % 2, NY),
            "rep_2": lax.rem(c + k % 2, NC),
        }

    def signal(sem, device):
        pl.semaphore_signal(sem, inc=1, device_id=device, device_id_type=MESH)

    barrier = pltpu.get_barrier_semaphore()
    for k in range(1, RANKS):
        signal(barrier, peer(k))

    @pl.when(head)
    def _():
        for device in [along(-3), along(-2), along(-1), beyond(0), beyond(-1), beyond(-2)]:
            signal(barrier, device)

    own = pl.ds(pl.multiple_of(rank * rows, rows), rows)
    own_shard = pl.ds(pl.multiple_of((yh * nz + z) * shard, shard), shard)
    fills = [
        pltpu.make_async_copy(m_ref, m_all.at[own], local_sem.at[0]),
        pltpu.make_async_copy(e_ref, e_all.at[own], local_sem.at[1]),
        pltpu.make_async_copy(h_ref, h_all.at[own_shard], local_sem.at[2]),
    ]
    for fill in fills:
        fill.start()

    def copy(src, dst, send_sem, recv_sem, device):
        return pltpu.make_async_remote_copy(
            src_ref=src, dst_ref=dst, send_sem=send_sem, recv_sem=recv_sem,
            device_id=device, device_id_type=MESH,
        )

    A, B = 0, 1

    def chip(cx, cy):
        return cx * NY + cy

    def index(cx, cy, piece):
        return piece * (NX * NY) + chip(cx, cy)

    def place(array, cx, cy, piece):
        return array.at[pl.ds(pl.multiple_of((cx * 4 + cy * 2 + piece) * rows, rows), rows)]

    def bulk_of(array, send_sem, recv, over, ahead, behind, xa, xb, turn):
        def here(cx, cy, piece, k):
            return place(array, cx, cy, piece).at[pl.ds(k * bit, bit)]

        def to(device, cx, cy, piece, k, src=None):
            at = here(cx, cy, piece, k)
            recv_sem = recv.at[index(cx, cy, piece) * BITS + k]
            copy(at if src is None else src.at[pl.ds(k * bit, bit)], at, send_sem, recv_sem, device).start()

        def got(cx, cy, piece, k):
            at = here(cx, cy, piece, k)
            copy(at, at, send_sem, recv.at[index(cx, cy, piece) * BITS + k], sibling).wait_recv()

        def step(cx, cy, piece, *devices):
            for k in range(BITS):
                got(cx, cy, piece, k)
                for device in devices:
                    to(device, cx, cy, piece, k)
                over(here(cx, cy, piece, k), cx, cy, piece)

        def first(source):
            for k in range(BITS):
                to(across, x, y, B, k, source)

        def start(source):
            for k in range(BITS):
                for device in (ahead, behind):
                    to(device, x, y, B, k, source)
            for k in range(BITS):
                got(x, y, A, k)
                for device in (ahead, behind, across):
                    to(device, x, y, A, k)

        def one():
            step(x, yo, B, ahead, behind)
            step(xa, y, B, behind)
            step(xb, y, B)
            step(xb, y, A, ahead, across)

        def two():
            step(xa, y, A, across)
            step(x, yo, A)
            step(xb, yo, B, ahead)
            step(xa, yo, B)

        def three():
            step(x2, y, B)
            step(x2, y, A, *(() if turn else (across,)))
            step(xb, yo, A, *((ahead,) if turn else ()))
            step(xa, yo, A)

        def four():
            step(x2, yo, B)
            step(x2, yo, A)

        return first, start, one, two, three, four

    def m_over(here, cx, cy, piece):
        copy(here, here, m_send, m_sib, sibling).start()

    def e_over(here, cx, cy, piece):
        if piece == A:
            copy(here, here, e_send, e_sib.at[chip(cx, cy)], sibling).start()

    def wait_sent(ref, sem, total):
        most = ref.shape[0]
        while total > 0:
            view = ref.at[pl.ds(0, min(total, most))]
            copy(view, view, sem, m_sib, sibling).wait_send()
            total -= most

    def wait_got(ref, sem, total):
        view = ref.at[pl.ds(0, total)]
        copy(view, view, m_send, sem, sibling).wait_recv()

    m_first, m_start, m_one, m_two, m_three, m_four = bulk_of(
        m_all, m_send, m_recv, m_over, plus, minus, xa, xb, False
    )
    e_first, e_start, e_one, e_two, e_three, e_four = bulk_of(
        e_all, e_send, e_recv, e_over, minus, plus, xb, xa, True
    )

    @pl.when(bulk)
    def _():
        pl.semaphore_wait(barrier, RANKS - 1)
        m_first(m_ref)
        m_start(m_ref)
        e_first(e_ref)
        e_start(e_ref)
        copy(m_ref, place(m_all, x, y, B), m_send, m_sib, sibling).start()
        m_one()
        e_one()
        m_two()
        e_two()
        m_three()
        e_three()
        m_four()
        e_four()

    def h_place(cy, cz):
        return h_all.at[pl.ds(pl.multiple_of((cy * nz + cz) * shard, shard), shard)]

    def h_to(device, recv, cy, cz, src=None):
        here = h_place(cy, cz)
        copy(here if src is None else src, here, h_send, recv.at[cz] if device is not sibling else recv, device).start()

    def h_got(recv, cy, d):
        here = h_place(cy, zat(d))
        copy(here, here, h_send, recv.at[zat(d)], sibling).wait_recv()

    def h_line(d, jumps, near):
        h_got(hz_recv, yh, d)
        cz = zat(d)
        for step in jumps:
            h_to(along(step), hz_recv, yh, cz)
        for step in near:
            h_to(along(step), hz_recv, yh, cz)
            h_to(beyond(step), hy_recv, yh, cz)
        h_to(beyond(0), hy_recv, yh, cz)
        h_to(sibling, h_sib, yh, cz)

    def h_leaf(*ds):
        for d in ds:
            h_got(hz_recv, yh, d)
            h_to(sibling, h_sib, yh, zat(d))

    def crossed(*ds):
        for d in ds:
            h_got(hy_recv, 1 - yh, d)
            h_to(sibling, h_sib, 1 - yh, zat(d))

    def give(source, array, send_sem, recv):
        for k in range(BITS):
            at = pl.ds(k * bit, bit)
            recv_sem = recv.at[index(x, y, A) * BITS + k]
            copy(source.at[at], place(array, x, y, A).at[at], send_sem, recv_sem, sibling).start()

    @pl.when(head)
    def _():
        pl.semaphore_wait(barrier, RANKS + 5)
        for device in [along(3), along(1), beyond(1)]:
            signal(ready, device)
        give(m_ref, m_all, m_send, m_recv)
        h_to(along(3), hz_recv, yh, z, h_ref)
        h_to(along(1), hz_recv, yh, z, h_ref)
        h_to(beyond(1), hy_recv, yh, z, h_ref)
        h_to(beyond(0), hy_recv, yh, z, h_ref)
        give(e_ref, e_all, e_send, e_recv)
        pl.semaphore_wait(ready, 3)
        h_to(along(-3), hz_recv, yh, z, h_ref)
        h_to(along(-1), hz_recv, yh, z, h_ref)
        h_to(beyond(-1), hy_recv, yh, z, h_ref)
        h_leaf(-1)
        h_line(-3, (3,), (1, -1))
        h_leaf(1)
        h_line(3, (-3,), (1, -1))
        crossed(0, -1, 1)
        h_leaf(-4, 2, 4, -2)
        h_line(-6, (), (2, 1, -1))
        crossed(-3, 3)
        h_line(6, (), (1, -1))
        crossed(-4, 2, 4, -2)
        h_leaf(-7, 5, 7, -5, 8)
        crossed(-6, 6, -7, 5, 7, -5, 8)

    for fill in fills:
        fill.wait()

    @pl.when(bulk)
    def _():
        wait_got(h_all, h_sib, (2 * nz - 1) * shard)

    def columns(n, size=CHUNK):
        return pl.ds(pl.multiple_of(n * size, size), size)

    def project(*chips):
        at = [pl.ds(pl.multiple_of((cx * 4 + cy * 2 + c) * rows, rows), rows) for cx, cy in chips]

        @pl.loop(0, width // CHUNK)
        def _(n):
            for block in at:
                p_all[block, columns(n)] = jnp.dot(
                    e_all[block, :], h_all[:, columns(n)], preferred_element_type=jnp.float32
                ).astype(jnp.bfloat16)

        for cx, cy in chips:
            here = place(p_all, cx, cy, c)
            copy(here, here, p_send, p_sib.at[chip(cx, cy)], sibling).start()

    project((x, y))

    @pl.when(head)
    def _():
        wait_got(m_all, m_sib, (RANKS - 1) * rows)

    @pl.loop(0, group // WIDE)
    def _(n):
        at = columns(n, WIDE)
        scores = scale * lax.dot_general(
            m_all[at, :], p_all[own, :], NT, preferred_element_type=jnp.float32
        ).T
        st[:, at] = scores
        top = jnp.max(scores, axis=0, keepdims=True)
        lse[rank, :, at] = top + jnp.log(jnp.sum(jnp.exp(scores - top), axis=0, keepdims=True))

    for k in range(1, RANKS):
        copy(lse.at[rank], lse.at[rank], st_send, st_recv.at[rank], peer(k)).start()

    others = [(x, yo), (xa, y), (xb, y), (x2, y), (xa, yo), (xb, yo), (x2, yo)]

    @pl.when(head)
    def _():
        for cx, cy in others:
            here = place(e_all, cx, cy, A)
            copy(here, here, e_send, e_sib.at[chip(cx, cy)], sibling).wait_recv()

    project(*others)
    for k in range(1, RANKS):
        device = peer(k)
        other = device["rep_0"] * 4 + device["rep_1"] * 2 + device["rep_2"]
        copy(lse.at[other], lse.at[other], st_send, st_recv.at[other], sibling).wait_recv()
    parts = lse[...]
    top = jnp.max(parts, axis=0)
    lt[...] = top + jnp.log(jnp.sum(jnp.exp(parts - top[None]), axis=0))

    @pl.loop(0, group // CHUNK)
    def _(n):
        at = columns(n)
        ct[:, at] = jnp.exp(st[:, at] - lt[:, at]).astype(jnp.bfloat16)

    block = st[:, own]
    diagonal = lax.broadcasted_iota(jnp.int32, block.shape, 0) == lax.broadcasted_iota(
        jnp.int32, block.shape, 1
    )
    own_total = lt[:, own]
    loss_ref[...] = own_total - jnp.sum(jnp.where(diagonal, block, 0.0), axis=0, keepdims=True)
    total_rows = jnp.broadcast_to(own_total, (rows, rows)).T[:, :1]

    @pl.loop(0, width // CHUNK)
    def _(n):
        total = jnp.dot(ct[...], m_all[:, columns(n)], preferred_element_type=jnp.float32)
        total = total - m_all[own, columns(n)].astype(jnp.float32)
        dp[:, columns(n)] = (scale * total).astype(jnp.bfloat16)

    @pl.loop(0, width // WIDE)
    def _(n):
        at = columns(n, WIDE)
        grad = lax.dot_general(h_all[at, :], dp[...], NT, preferred_element_type=jnp.float32)
        sg_ref[:, at] = grad.T.astype(jnp.bfloat16)

    for cx, cy in [(x, y)] + others:
        here = place(p_all, cx, cy, co)
        copy(here, here, p_send, p_sib.at[chip(cx, cy)], sibling).wait_recv()

    @pl.loop(0, group // WIDE)
    def _(n):
        at = columns(n, WIDE)
        scores = scale * lax.dot_general(
            p_all[at, :], m_all[own, :], NT, preferred_element_type=jnp.float32
        ).T
        ct[:, at] = jnp.exp(scores - total_rows).astype(jnp.bfloat16)

    @pl.loop(0, width // CHUNK)
    def _(n):
        total = jnp.dot(ct[...], p_all[:, columns(n)], preferred_element_type=jnp.float32)
        total = total - p_all[own, columns(n)].astype(jnp.float32)
        mg_ref[:, columns(n)] = (scale * total).astype(jnp.bfloat16)

    moves = 6 + 4 + 2 + 1 + 1

    @pl.when(bulk)
    def _():
        wait_sent(m_all, m_send, (moves + RANKS - 1) * rows)
        wait_sent(e_all, e_send, (moves + NX * NY - 1) * rows)

    @pl.when(head)
    def _():
        wait_sent(m_all, m_send, rows)
        wait_sent(e_all, e_send, rows)
        wait_sent(h_all, h_send, (7 + 7 + 7 + 8 + 6 + 11 + nz) * shard)

    wait_sent(p_all, p_send, NX * NY * rows)
    view = lse.at[pl.ds(0, RANKS - 1)]
    copy(view, view, st_send, m_sib, sibling).wait_send()


def local(nz, mentions, entity_states, head):
    rows, width = mentions.shape
    group = rows * RANKS
    bf16, f32 = jnp.bfloat16, jnp.float32
    pieces = 2 * NX * NY
    dma = pltpu.SemaphoreType.DMA
    any_spec = pl.BlockSpec(memory_space=pl.ANY)
    vmem_spec = pl.BlockSpec(memory_space=pltpu.VMEM)
    loss, mention_grad, state_grad = pl.pallas_call(
        functools.partial(kernel, nz, 3.0 / math.sqrt(width)),
        out_shape=(
            pltpu.VMEM((1, rows), f32),
            pltpu.VMEM((rows, width), bf16),
            pltpu.VMEM((rows, width), bf16),
        ),
        in_specs=[any_spec] * 3,
        out_specs=(vmem_spec,) * 3,
        scratch_shapes=[
            pltpu.VMEM((group, width), bf16),
            pltpu.VMEM((group, width), bf16),
            pltpu.VMEM((group, width), bf16),
            pltpu.VMEM((width, width), bf16),
            pltpu.VMEM((rows, group), f32),
            pltpu.VMEM((rows, group), bf16),
            pltpu.VMEM((RANKS, 1, group), f32),
            pltpu.VMEM((1, group), f32),
            pltpu.VMEM((rows, width), bf16),
            dma((3,)),
            dma((pieces * BITS,)),
            dma,
            dma((pieces * BITS,)),
            dma((NX * NY,)),
            dma((NX * NY,)),
            dma((nz,)),
            dma((nz,)),
            dma,
            dma((RANKS,)),
            dma, dma, dma, dma, dma,
            pltpu.SemaphoreType.REGULAR,
        ],
        compiler_params=pltpu.CompilerParams(collective_id=0, has_side_effects=True),
    )(mentions, entity_states, head)
    return loss.reshape(rows), mention_grad, state_grad


def solution(mesh):
    torus = Mesh(mesh.devices.reshape(2, 16, 4, 2, 2), DP_REP)
    in_specs = (P(DP_REP, None), P(DP_REP, None), P(("dp_0", "dp_1"), None))
    out_specs = (P(DP_REP), P(DP_REP, None), P(DP_REP, None))
    return jax.shard_map(
        functools.partial(local, 16), mesh=torus, in_specs=in_specs, out_specs=out_specs, check_vma=False
    )
```
